256 devices in a mesh: pts: 128 (over x, y, z), rep: 2 (over core).
Axes of the slice: x: 4, y: 4, z: 8, core: 2. Of those that a mesh axis runs over, the one named last changes fastest.
Arguments:
- points: float32 [3, 524288], P(None, ('pts', 'rep')), may hold values from 0 to 1
- scales: float32 [3], replicated, may hold values from 0.1 to 0.3
- pivots: int32 [4, 128], replicated, may hold values from 0 to 524287, as said below
Outputs:
- factor: float32 [512, 524288], P(None, ('pts', 'rep'))
The draws below stay inside these ranges and needn't reach their ends.
Inputs may be any that keep to these rules, and one draw needn't show every extreme that they name: All 512 indices are distinct. Point i lies on the device whose flat index over pts+rep is i // 2048; no device holds more than 2 pivots of one round, and some device holds exactly 2 in every round.
All inputs are finite; a program needn't handle non-finite values.
Results may differ from the reference program's by a relative error of at most 0.0003.
Values sent between devices are 32-bit elements; how exact they have to be, the bound alone decides.
No kernel may reach another device: no remote copies, remote signals or barrier semaphores. Data moves between devices by JAX's collectives and lax.ppermute only.
A program may use at most 64 MiB of HBM per device.

```python
import math
import jax
import jax.numpy as jnp
from jax import lax

DIM = 3
B = 128
R = 4
P_DEV = 2048
NPTS = 524288
CAP = 2


def draw_pivots(key, part):
    device_list = NPTS // P_DEV
    every_slot = device_list * CAP
    order_keys = jax.random.split(jax.random.fold_in(key, 7), device_list)
    orders = jax.vmap(lambda order_key: jax.random.permutation(order_key, P_DEV))(order_keys)
    listed = []
    for round_index in range(R):
        round_seed_key = jax.random.fold_in(key, 100 + round_index)
        heaviest_key, extra_weight_key, jitter_key, permute_key = jax.random.split(round_seed_key, 4)
        heaviest_device = jax.random.randint(heaviest_key, (), 0, device_list)
        extra_weight = jax.random.randint(extra_weight_key, (device_list,), 0, 4)
        extra_weight = jnp.where(jnp.arange(device_list) == heaviest_device, 4, extra_weight)
        jitter_values = jax.random.randint(jitter_key, (every_slot,), 0, 2 ** 18)
        slot_owner_device = jnp.arange(every_slot) // CAP
        device_scores = (jitter_values + extra_weight[slot_owner_device] * 2 ** 18) * every_slot + jnp.arange(every_slot)
        unused, picked = lax.top_k(device_scores, B)
        device_of = picked // CAP
        slot_of = picked % CAP
        local_index = orders[device_of, round_index * CAP + slot_of]
        indices = device_of * P_DEV + local_index
        listed.append(jax.random.permutation(permute_key, indices))
    return jnp.stack(listed).astype(jnp.int32)


def shard_levels(own_key, dims, cuts, smallest, high):
    def one(axis_at, parts):
        draws = jax.random.uniform(jax.random.fold_in(jax.random.fold_in(own_key, 6), axis_at), (parts,), jnp.float32, smallest / len(cuts), high / len(cuts))
        return jnp.repeat(jnp.exp(draws), dims[axis_at] // parts).reshape((-1,) + (1,) * (len(dims) - axis_at - 1))

    level = one(*cuts[0])
    for cut in cuts[1:]:
        level = level * one(*cut)
    return level


def setup_inputs(seed: int = 0) -> dict:
    keys = jax.random.split(jax.random.key(seed), 4)
    return {
        "points": jnp.clip(1.0 * jax.random.uniform(keys[0], (DIM, NPTS), jnp.float32) ** shard_levels(keys[0], (DIM, NPTS), ((1, 256),), -0.2, 0.2), 0.0, 1.0),
        "scales": jnp.clip(jnp.exp(jax.random.uniform(keys[1], (DIM,), jnp.float32, math.log(0.1), math.log(0.3))), 0.1, 0.3),
        "pivots": draw_pivots(jax.random.fold_in(keys[3], 71), 0),
    }


nugget_level = 0.1

def kernel_block(anchors, targets, inverse):
    squared = jnp.zeros((anchors.shape[1], targets.shape[1]), jnp.float32)
    for component in range(anchors.shape[0]):
        offset = (anchors[component][:, None] - targets[component][None, :]) * inverse[component]
        squared = squared + offset * offset
    return jnp.exp(-0.5 * squared)

def reference(points, scales, pivots):
    inverse = 1.0 / scales
    identity = jnp.eye(B, dtype=jnp.float32)
    blocks = []
    for round_index in range(R):
        chosen = pivots[round_index]
        anchors = points[:, chosen]
        residual = kernel_block(anchors, anchors, inverse) + nugget_level * identity
        columns = kernel_block(anchors, points, inverse)
        for earlier in blocks:
            earlier_rows = earlier[:, chosen]
            residual = residual - jnp.dot(earlier_rows.T, earlier_rows, precision=lax.Precision.HIGHEST)
            columns = columns - jnp.dot(earlier_rows.T, earlier, precision=lax.Precision.HIGHEST)
        factor = jnp.linalg.cholesky(residual)
        blocks.append(lax.linalg.triangular_solve(factor, columns, left_side=True, lower=True))
    return jnp.concatenate(blocks, axis=0)
```

```python
import functools
import math

import jax
import jax.numpy as jnp
from jax import lax
from jax.experimental import pallas as pl
from jax.experimental.pallas import tpu as pltpu
from jax.sharding import PartitionSpec as P

nugget_level = 0.1
root_factor = math.sqrt(0.5 * math.log2(math.e))
f32 = jnp.float32
bf16 = jnp.bfloat16
HIGHEST = lax.Precision.HIGHEST


def iota(shape, axis):
    return lax.broadcasted_iota(jnp.int32, shape, axis)


def across_lanes(x, j):
    return jnp.broadcast_to(x[:, j : j + 1], (8, 128))


def across_rows(x, k):
    return jnp.broadcast_to(x[k : k + 1, :], (8, 128))


def pack_kernel(place_ref, points_ref, pivots_ref, out_ref):
    point_count = points_ref.shape[1]
    base = place_ref[0] * point_count
    sub, lane = iota((8, 128), 0), iota((8, 128), 1)
    spread = jnp.zeros((8, 128), jnp.int32)
    for round_index in range(pivots_ref.shape[0]):
        row = jnp.broadcast_to(pivots_ref[round_index : round_index + 1, :], (8, 128))
        spread = jnp.where(sub // 2 == round_index, row, spread)
    local = spread - base
    owned = (local >= 0) & (local < point_count)
    first = jnp.min(jnp.where(owned, lane, 128), axis=1, keepdims=True)
    last = jnp.max(jnp.where(owned, lane, -1), axis=1, keepdims=True)
    second = jnp.where(last > first, last, -1)
    place = jnp.where(sub[:, :1] % 2 == 0, jnp.where(first < 128, first, -1), second)
    here = jnp.sum(jnp.where(lane == place, local, 0), axis=1, keepdims=True)
    columns = iota((8, point_count), 1)
    match = columns == here
    row = jnp.where(lane == 4 * sub + 3, place.astype(f32), 0.0)
    for c in range(points_ref.shape[0]):
        value = jnp.sum(jnp.where(match, points_ref[c : c + 1, :], 0.0), axis=1, keepdims=True)
        row = jnp.where(lane == 4 * sub + c, value, row)
    row = jnp.sum(row, axis=0, keepdims=True)
    out_ref[...] = jnp.broadcast_to(row, out_ref.shape)


def split3(x):
    a = x.astype(bf16).astype(f32)
    rest = x - a
    b = rest.astype(bf16).astype(f32)
    return a, b, rest - b


def eliminate(groups):
    sub, lane = iota((8, 128), 0), iota((8, 128), 1)
    groups = list(groups)
    count = len(groups)
    for b in range(count):
        column = [across_lanes(groups[b], 8 * b + k) for k in range(8)]
        follows = b < count - 1
        inside = (lane >= 8 * b) & (lane < 8 * b + 8)
        rows = jnp.where(inside, jnp.where(lane - 8 * b == sub, 1.0, 0.0).astype(f32), groups[b])
        if follows:
            lower = [across_lanes(groups[b + 1], 8 * b + k) for k in range(8)]
            after = jnp.where(inside, 0.0, groups[b + 1])
        for k in range(8):
            scale = lax.rsqrt(across_rows(column[k], k))
            below = jnp.where(sub > k, column[k] * scale, 0.0)
            pivot_row = across_rows(rows, k) * scale
            factor = {}
            for m in range(k + 1, 8):
                factor[m] = across_rows(column[m], k) * scale
                column[m] = column[m] - below * factor[m]
            rows = jnp.where(sub == k, pivot_row, rows - below * pivot_row)
            if follows:
                multiplier = lower[k] * scale
                for m in range(k + 1, 8):
                    lower[m] = lower[m] - multiplier * factor[m]
                after = after - multiplier * pivot_row
        groups[b] = rows
        if follows:
            groups[b + 1] = after
        if b < count - 2:
            r1, r2, r3 = split3(rows)
            left = jnp.concatenate([r1, r1, r2, r2, r1, r3], 0).astype(bf16)
            right = jnp.concatenate([r1, r2, r1, r2, r3, r1], 0).astype(bf16)
            update = lax.dot_general(
                left, right, (((0,), (0,)), ((), ())), preferred_element_type=f32
            )
            for g in range(b + 2, count):
                groups[g] = jnp.where(inside, 0.0, groups[g]) - update[8 * g : 8 * g + 8, :]
    return groups


def main_kernel(gathered_ref, points_ref, scales_ref, out_ref, matrix, high, low, tall):
    dims, point_count = points_ref.shape
    pivot_count = 128
    rounds = out_ref.shape[0] // pivot_count
    total = rounds * pivot_count
    weights = [root_factor / jnp.full((1, 128), scales_ref[c], f32) for c in range(dims)]
    flipped = jnp.transpose(gathered_ref[...])
    anchor_rows, anchor_columns = [], []
    for r in range(rounds):
        wide = jnp.zeros((4, pivot_count), f32)
        for s in (2 * r, 2 * r + 1):
            fields = flipped[4 * s : 4 * s + 4, :]
            hot = jnp.where(
                fields[3:4, :] == iota((pivot_count, fields.shape[1]), 0).astype(f32), 1.0, 0.0
            ).astype(f32)
            wide = wide + lax.dot_general(
                fields, hot, (((1,), (1,)), ((), ())), precision=HIGHEST, preferred_element_type=f32
            )
        scaled = jnp.concatenate(
            [wide[c : c + 1, :] * weights[c] for c in range(dims)] + [jnp.zeros((5, 128), f32)], 0
        )
        anchor_rows.append(scaled)
        stood = jnp.transpose(jnp.concatenate([scaled] + [jnp.zeros((120, 128), f32)], 0))
        anchor_columns.append(stood[:, :8])
        tall[128 * r : 128 * r + 128, :] = stood[:, :8]

    for r in range(rounds):
        for t in range(r, rounds):
            squared = jnp.zeros((128, 128), f32)
            for c in range(dims):
                offset = anchor_columns[r][:, c : c + 1] - anchor_rows[t][c : c + 1, :]
                squared = squared + offset * offset
            block = jnp.exp2(-squared)
            if t == r:
                diagonal = iota((128, 128), 0) == iota((128, 128), 1)
                block = jnp.where(diagonal, block + nugget_level, block)
            matrix[128 * r : 128 * r + 128, 128 * t : 128 * t + 128] = block
        for t in range(r):
            matrix[128 * r : 128 * r + 128, 128 * t : 128 * t + 128] = jnp.zeros((128, 128), f32)

    keep = iota((128, 128), 0) >= iota((128, 128), 1)
    for r in range(rounds):
        lo, hi = 128 * r, 128 * r + 128
        groups = eliminate([matrix[lo + 8 * g : lo + 8 * g + 8, lo:hi] for g in range(16)])
        inverse = jnp.where(keep, jnp.concatenate(groups, 0), 0.0)
        solved = jnp.dot(inverse, matrix[lo:hi, :], precision=HIGHEST, preferred_element_type=f32)
        matrix[lo:hi, :] = solved
        matrix[lo:hi, lo:hi] = inverse
        for t in range(r + 1, rounds):
            lt, ht = 128 * t, 128 * t + 128
            matrix[lt:ht, lo:hi] = jnp.zeros((128, 128), f32)
            matrix[lt:ht, :] = matrix[lt:ht, :] - lax.dot_general(
                matrix[lo:hi, lt:ht],
                matrix[lo:hi, :],
                (((0,), (0,)), ((), ())),
                precision=HIGHEST,
                preferred_element_type=f32,
            )
    for r in range(rounds):
        lo, hi = 128 * r, 128 * r + 128
        part = matrix[lo:hi, :hi]
        top = part.astype(bf16)
        high[lo:hi, :hi] = top
        low[lo:hi, :hi] = (part - top.astype(f32)).astype(bf16)

    step = 256

    def chunk(i, _):
        at = pl.multiple_of(i * step, step)
        here = [points_ref[c : c + 1, pl.ds(at, step)] * weights[c][:, :1] for c in range(dims)]
        tops, rests = [], []
        for r in range(rounds):
            lo, hi = 128 * r, 128 * r + 128
            squared = jnp.zeros((128, step), f32)
            for c in range(dims):
                offset = tall[lo:hi, c : c + 1] - here[c]
                squared = squared + offset * offset
            value = jnp.exp2(-squared)
            top = value.astype(bf16)
            tops.append(top)
            rests.append((value - top.astype(f32)).astype(bf16))
            k_top = jnp.concatenate(tops, 0)
            k_rest = jnp.concatenate(rests, 0)
            h, l = high[lo:hi, :hi], low[lo:hi, :hi]
            out_ref[lo:hi, pl.ds(at, step)] = (
                jnp.dot(h, k_top, preferred_element_type=f32)
                + jnp.dot(h, k_rest, preferred_element_type=f32)
                + jnp.dot(l, k_top, preferred_element_type=f32)
            )
        return 0

    lax.fori_loop(0, point_count // step, chunk, 0)


def per_device(points, scales, pivots):
    devices = lax.axis_size(("pts", "rep"))
    dims, point_count = points.shape
    rounds, pivot_count = pivots.shape
    place = lax.axis_index(("pts", "rep")).astype(jnp.int32).reshape(1)
    vmem, smem = pl.BlockSpec(memory_space=pltpu.VMEM), pl.BlockSpec(memory_space=pltpu.SMEM)
    packed = pl.pallas_call(
        pack_kernel,
        out_shape=jax.ShapeDtypeStruct((devices, 128), f32),
        in_specs=[smem, vmem, vmem],
        out_specs=vmem,
    )(place, points, pivots)
    gathered = lax.all_to_all(packed, ("pts", "rep"), 0, 0, tiled=True)
    total = rounds * pivot_count
    return pl.pallas_call(
        main_kernel,
        out_shape=jax.ShapeDtypeStruct((total, point_count), f32),
        in_specs=[vmem, vmem, smem],
        out_specs=vmem,
        scratch_shapes=[
            pltpu.VMEM((total, total), f32),
            pltpu.VMEM((total, total), bf16),
            pltpu.VMEM((total, total), bf16),
            pltpu.VMEM((total, 8), f32),
        ],
    )(gathered, points, scales)


def solution(mesh):
    placed = (P(None, ("pts", "rep")), P(), P())
    return jax.shard_map(
        per_device, mesh=mesh, in_specs=placed, out_specs=P(None, ("pts", "rep")), check_vma=False
    )
```

```python
import functools
import math

import jax
import jax.numpy as jnp
from jax import lax
from jax.experimental import pallas as pl
from jax.experimental.pallas import tpu as pltpu
from jax.sharding import PartitionSpec as P

nugget_level = 0.1
root_factor = math.sqrt(0.5 * math.log2(math.e))
f32 = jnp.float32
bf16 = jnp.bfloat16
HIGHEST = lax.Precision.HIGHEST


def iota(shape, axis):
    return lax.broadcasted_iota(jnp.int32, shape, axis)


def across_lanes(x, j):
    return jnp.broadcast_to(x[:, j : j + 1], (8, 128))


def across_rows(x, k):
    return jnp.broadcast_to(x[k : k + 1, :], (8, 128))


def pack_kernel(place_ref, points_ref, pivots_ref, out_ref):
    point_count = points_ref.shape[1]
    base = place_ref[0] * point_count
    sub, lane = iota((8, 128), 0), iota((8, 128), 1)
    spread = jnp.zeros((8, 128), jnp.int32)
    for round_index in range(pivots_ref.shape[0]):
        row = jnp.broadcast_to(pivots_ref[round_index : round_index + 1, :], (8, 128))
        spread = jnp.where(sub // 2 == round_index, row, spread)
    local = spread - base
    owned = (local >= 0) & (local < point_count)
    first = jnp.min(jnp.where(owned, lane, 128), axis=1, keepdims=True)
    last = jnp.max(jnp.where(owned, lane, -1), axis=1, keepdims=True)
    second = jnp.where(last > first, last, -1)
    place = jnp.where(sub[:, :1] % 2 == 0, jnp.where(first < 128, first, -1), second)
    here = jnp.sum(jnp.where(lane == place, local, 0), axis=1, keepdims=True)
    columns = iota((8, point_count), 1)
    match = columns == here
    row = jnp.where(lane == 4 * sub + 3, place.astype(f32), 0.0)
    for c in range(points_ref.shape[0]):
        value = jnp.sum(jnp.where(match, points_ref[c : c + 1, :], 0.0), axis=1, keepdims=True)
        row = jnp.where(lane == 4 * sub + c, value, row)
    row = jnp.sum(row, axis=0, keepdims=True)
    out_ref[...] = jnp.broadcast_to(row, out_ref.shape)


def split3(x):
    a = x.astype(bf16).astype(f32)
    rest = x - a
    b = rest.astype(bf16).astype(f32)
    return a, b, rest - b


def eliminate(groups):
    sub, lane = iota((8, 128), 0), iota((8, 128), 1)
    count = len(groups)
    for b in range(count):
        column = [across_lanes(groups[b], 8 * b + k) for k in range(8)]
        follows = b < count - 1
        inside = (lane >= 8 * b) & (lane < 8 * b + 8)
        rows = jnp.where(inside, jnp.where(lane - 8 * b == sub, 1.0, 0.0).astype(f32), groups[b])
        final = rows
        if follows:
            lower = [across_lanes(groups[b + 1], 8 * b + k) for k in range(8)]
            after = jnp.where(inside, 0.0, groups[b + 1])
        for k in range(0, 8, 2):
            a = across_rows(column[k], k)
            side = across_rows(column[k], k + 1)
            c = across_rows(column[k + 1], k + 1)
            root = lax.rsqrt(a * c - side * side)
            scale = root * root
            masked0 = jnp.where(sub > k + 1, column[k], 0.0)
            masked1 = jnp.where(sub > k + 1, column[k + 1], 0.0)
            raw0 = masked0 * c - masked1 * side
            raw1 = masked1 * a - masked0 * side
            below0, below1 = raw0 * scale, raw1 * scale
            picks = {}
            for m in range(k + 2, 8):
                picks[m] = (across_rows(column[k], m), across_rows(column[k + 1], m))
                p0, p1 = picks[m]
                if m < k + 4:
                    column[m] = column[m] - (raw0 * p0 + raw1 * p1) * scale
                else:
                    column[m] = column[m] - (below0 * p0 + below1 * p1)
            row0, row1 = across_rows(rows, k), across_rows(rows, k + 1)
            if follows:
                next0 = (lower[k] * c - lower[k + 1] * side) * scale
                next1 = (lower[k + 1] * a - lower[k] * side) * scale
                for m in range(k + 2, 8):
                    p0, p1 = picks[m]
                    lower[m] = lower[m] - (next0 * p0 + next1 * p1)
                after = after - (next0 * row0 + next1 * row1)
            if k < 6:
                rows = rows - (below0 * row0 + below1 * row1)
            first = lax.rsqrt(a)
            ratio = side * (first * first)
            final = jnp.where(sub == k, row0 * first, final)
            final = jnp.where(sub == k + 1, (row1 - row0 * ratio) * (root * (a * first)), final)
            if follows and k == 6:
                groups[b + 1] = after
            yield
        groups[b] = final
        if b < count - 2:
            r1, r2, r3 = split3(final)
            left = jnp.concatenate([r1, r1, r2, r2, r1, r3], 0).astype(bf16)
            right = jnp.concatenate([r1, r2, r1, r2, r3, r1], 0).astype(bf16)
            update = lax.dot_general(
                left, right, (((0,), (0,)), ((), ())), preferred_element_type=f32
            )
            for g in range(b + 2, count):
                groups[g] = jnp.where(inside, 0.0, groups[g]) - update[8 * g : 8 * g + 8, :]


def split2(x):
    top = x.astype(bf16)
    return top, (x - top.astype(f32)).astype(bf16)


def squares(columns, rows):
    total = None
    for c in range(3):
        offset = columns[:, c : c + 1] - rows[c]
        total = offset * offset if total is None else total + offset * offset
    return total


def outer(left, right):
    return lax.dot_general(
        left, right, (((0,), (0,)), ((), ())), precision=HIGHEST, preferred_element_type=f32
    )


def main_kernel(
    gathered_ref, points_ref, scales_ref, out_ref, matrix, near, tall, solved, stack, ready, lows, done
):
    dims, point_count = points_ref.shape
    rounds = out_ref.shape[0] // 128
    step = 256
    chunks = point_count // step
    weights = [root_factor / jnp.full((1, 128), scales_ref[c], f32) for c in range(dims)]
    flipped = jnp.transpose(gathered_ref[...])
    anchors = []
    for r in range(rounds):
        wide = jnp.zeros((16, 128), f32)
        for s in (2 * r, 2 * r + 1):
            fields = flipped[4 * s : 4 * s + 4, :]
            places = iota((128, fields.shape[1]), 0).astype(f32)
            hot = jnp.where(fields[3:4, :] == places, 1.0, 0.0).astype(bf16)
            parts = split3(fields)
            parts = jnp.concatenate(list(parts) + [parts[0]], 0).astype(bf16)
            wide = wide + lax.dot_general(
                parts, hot, (((1,), (1,)), ((), ())), preferred_element_type=f32
            )
        wide = (wide[0:4, :] + wide[4:8, :]) + wide[8:12, :]
        scaled = jnp.concatenate(
            [wide[c : c + 1, :] * weights[c] for c in range(dims)] + [jnp.zeros((5, 128), f32)], 0
        )
        anchors.append([scaled[c : c + 1, :] for c in range(dims)])
        tall[128 * r : 128 * r + 128, :] = jnp.transpose(
            jnp.concatenate([scaled] + [jnp.zeros((120, 128), f32)], 0)
        )[:, :8]
    for c in range(dims):
        near[c : c + 1, :] = points_ref[c : c + 1, :] * weights[c][:, :1]

    def fill(r, t):
        block = jnp.exp2(-squares(tall[128 * r : 128 * r + 128, :], anchors[t]))
        if t == r:
            diagonal = iota((128, 128), 0) == iota((128, 128), 1)
            block = jnp.where(diagonal, block + nugget_level, block)
        matrix[128 * r : 128 * r + 128, 128 * t : 128 * t + 128] = block

    def block(r, t):
        return matrix[128 * r : 128 * r + 128, 128 * t : 128 * t + 128]

    def columns_task(r, j, part):
        span = slice(j * step, j * step + step)
        size = 128 // 4
        lo = size * part
        value = jnp.exp2(
            -squares(
                tall[128 * r + lo : 128 * r + lo + size, :],
                [near[c : c + 1, span] for c in range(dims)],
            )
        )
        if r > 0:
            value = value - jnp.dot(
                lows[lo : lo + size, 384 * OFFSET[r] : 384 * (OFFSET[r] + r)],
                stack[: 384 * r, span],
                preferred_element_type=f32,
            )
        top, rest = split2(value)
        ready[lo : lo + size, span] = top
        ready[128 + lo : 128 + lo + size, span] = rest
        ready[256 + lo : 256 + lo + size, span] = top

    def solve_task(r, j, inverses):
        span = slice(j * step, j * step + step)
        value = jnp.dot(inverses, ready[:, span], preferred_element_type=f32)
        solved[128 * r : 128 * r + 128, span] = value
        if r < rounds - 1:
            top, rest = split2(value)
            stack[384 * r : 384 * r + 128, span] = top
            stack[384 * r + 128 : 384 * r + 256, span] = rest
            stack[384 * r + 256 : 384 * r + 384, span] = top

    def copy_out(r):
        return pltpu.make_async_copy(
            solved.at[pl.ds(128 * r, 128), :], out_ref.at[pl.ds(128 * r, 128), :], done.at[r]
        )

    def flip_task(s, t):
        top, rest = split2(jnp.transpose(block(s, t)))
        at = 384 * (OFFSET[t] + s)
        lows[:, at : at + 128] = top
        lows[:, at + 128 : at + 256] = top
        lows[:, at + 256 : at + 384] = rest

    def subtract_task(s, t, u):
        matrix[128 * t : 128 * t + 128, 128 * u : 128 * u + 128] = block(t, u) - outer(
            block(s, t), block(s, u)
        )

    keep = iota((128, 128), 0) >= iota((128, 128), 1)
    fill(0, 0)
    inverse = inverses = None
    for r in range(rounds):
        tasks = []
        if r == 0:
            tasks += [functools.partial(fill, t, u) for t in range(rounds) for u in range(t, rounds) if u]
        else:
            s = r - 1
            for u in range(r + 1, rounds):
                tasks.append(functools.partial(widen, s, u, inverse))
            tasks += [functools.partial(flip_task, s, t) for t in range(r, rounds)]
            tasks += [
                functools.partial(subtract_task, s, t, u)
                for t in range(r, rounds)
                for u in range(t, rounds)
                if u > r
            ]
        for j in range(chunks):
            if r > 0:
                tasks.append(functools.partial(solve_task, r - 1, j, inverses))
            for part in range(4):
                tasks.append(functools.partial(columns_task, r, j, part))
        groups = [matrix[128 * r + 8 * g : 128 * r + 8 * g + 8, 128 * r : 128 * r + 128] for g in range(16)]
        at, slots = 0, 64
        for slot, _ in enumerate(eliminate(groups)):
            until = (slot + 1) * len(tasks) // slots
            while at < until:
                tasks[at]()
                at += 1
        inverse = jnp.where(keep, jnp.concatenate(groups, 0), 0.0)
        top, rest = split2(inverse)
        inverses = jnp.concatenate([top, top, rest], 1)

        def widen(s, u, inverse):
            matrix[128 * s : 128 * s + 128, 128 * u : 128 * u + 128] = jnp.dot(
                inverse, block(s, u), precision=HIGHEST, preferred_element_type=f32
            )

        if r > 0:
            copy_out(r - 1).start()
        if r < rounds - 1:
            widen(r, r + 1, inverse)
            subtract_task(r, r + 1, r + 1)
    for j in range(chunks):
        solve_task(rounds - 1, j, inverses)
    copy_out(rounds - 1).start()
    for r in range(rounds):
        copy_out(r).wait()


OFFSET = [0, 0, 1, 3]


def per_device(points, scales, pivots):
    devices = lax.axis_size(("pts", "rep"))
    dims, point_count = points.shape
    rounds, pivot_count = pivots.shape
    place = lax.axis_index(("pts", "rep")).astype(jnp.int32).reshape(1)
    vmem, smem = pl.BlockSpec(memory_space=pltpu.VMEM), pl.BlockSpec(memory_space=pltpu.SMEM)
    packed = pl.pallas_call(
        pack_kernel,
        out_shape=jax.ShapeDtypeStruct((devices, 128), f32),
        in_specs=[smem, vmem, vmem],
        out_specs=vmem,
    )(place, points, pivots)
    gathered = lax.all_to_all(packed, ("pts", "rep"), 0, 0, tiled=True)
    total = rounds * pivot_count
    return pl.pallas_call(
        main_kernel,
        out_shape=jax.ShapeDtypeStruct((total, point_count), f32),
        in_specs=[vmem, vmem, smem],
        out_specs=pl.BlockSpec(memory_space=pl.ANY),
        scratch_shapes=[
            pltpu.VMEM((total, total), f32),
            pltpu.VMEM((8, point_count), f32),
            pltpu.VMEM((total, 8), f32),
            pltpu.VMEM((total, point_count), f32),
            pltpu.VMEM((384 * (rounds - 1), point_count), bf16),
            pltpu.VMEM((384, point_count), bf16),
            pltpu.VMEM((128, 384 * 6), bf16),
            pltpu.SemaphoreType.DMA((rounds,)),
        ],
    )(gathered, points, scales)


def solution(mesh):
    placed = (P(None, ("pts", "rep")), P(), P())
    return jax.shard_map(
        per_device, mesh=mesh, in_specs=placed, out_specs=P(None, ("pts", "rep")), check_vma=False
    )
```

```python
import functools
import math

import jax
import jax.numpy as jnp
from jax import lax
from jax.experimental import pallas as pl
from jax.experimental.pallas import tpu as pltpu
from jax.sharding import PartitionSpec as P

nugget_level = 0.1
root_factor = math.sqrt(0.5 * math.log2(math.e))
f32 = jnp.float32
bf16 = jnp.bfloat16
HIGHEST = lax.Precision.HIGHEST


def iota(shape, axis):
    return lax.broadcasted_iota(jnp.int32, shape, axis)


def across_lanes(x, j):
    return jnp.broadcast_to(x[:, j : j + 1], (8, 128))


def across_rows(x, k):
    return jnp.broadcast_to(x[k : k + 1, :], (8, 128))


def pack_kernel(place_ref, points_ref, pivots_ref, out_ref):
    point_count = points_ref.shape[1]
    base = place_ref[0] * point_count
    sub, lane = iota((8, 128), 0), iota((8, 128), 1)
    spread = jnp.zeros((8, 128), jnp.int32)
    for round_index in range(pivots_ref.shape[0]):
        row = jnp.broadcast_to(pivots_ref[round_index : round_index + 1, :], (8, 128))
        spread = jnp.where(sub // 2 == round_index, row, spread)
    local = spread - base
    owned = (local >= 0) & (local < point_count)
    first = jnp.min(jnp.where(owned, lane, 128), axis=1, keepdims=True)
    last = jnp.max(jnp.where(owned, lane, -1), axis=1, keepdims=True)
    second = jnp.where(last > first, last, -1)
    place = jnp.where(sub[:, :1] % 2 == 0, jnp.where(first < 128, first, -1), second)
    here = jnp.sum(jnp.where(lane == place, local, 0), axis=1, keepdims=True)
    columns = iota((8, point_count), 1)
    match = columns == here
    row = jnp.where(lane == 4 * sub + 3, place.astype(f32), 0.0)
    for c in range(points_ref.shape[0]):
        value = jnp.sum(jnp.where(match, points_ref[c : c + 1, :], 0.0), axis=1, keepdims=True)
        row = jnp.where(lane == 4 * sub + c, value, row)
    row = jnp.sum(row, axis=0, keepdims=True)
    out_ref[...] = jnp.broadcast_to(row, out_ref.shape)


def split3(x):
    a = x.astype(bf16).astype(f32)
    rest = x - a
    b = rest.astype(bf16).astype(f32)
    return a, b, rest - b


def total_of(terms):
    while len(terms) > 1:
        terms = [a + b for a, b in zip(terms[::2], terms[1::2])]
    return terms[0]
def eliminate(groups):
    sub, lane = iota((8, 128), 0), iota((8, 128), 1)
    odd = sub % 2 == 1
    pair = sub // 2
    count = len(groups)
    for b in range(count):
        column = [across_lanes(groups[b], 8 * b + k) for k in range(8)]
        follows = b < count - 1
        inside = (lane >= 8 * b) & (lane < 8 * b + 8)
        rows = jnp.where(inside, jnp.where(lane - 8 * b == sub, 1.0, 0.0).astype(f32), groups[b])
        if follows:
            lower = [across_lanes(groups[b + 1], 8 * b + k) for k in range(8)]
            after = jnp.where(inside, 0.0, groups[b + 1])
        final = rows
        coefs = []
        for k in range(0, 8, 2):
            mine = pair == k // 2
            a = across_rows(column[k], k)
            side = across_rows(column[k], k + 1)
            c = across_rows(column[k + 1], k + 1)
            root = lax.rsqrt(a * c - side * side)
            scale = root * root
            masked0 = jnp.where(mine, 0.0, column[k])
            masked1 = jnp.where(mine, 0.0, column[k + 1])
            raw0 = masked0 * c - masked1 * side
            raw1 = masked1 * a - masked0 * side
            part0, part1 = raw0 * scale, raw1 * scale
            coefs.append((a * scale, side * scale, c * scale))
            picks = {m: (across_rows(column[k], m), across_rows(column[k + 1], m)) for m in range(k + 2, 8)}
            for m in range(k + 2, 8):
                p0, p1 = picks[m]
                if m < k + 4:
                    column[m] = column[m] - (raw0 * p0 + raw1 * p1) * scale
                else:
                    column[m] = column[m] - (part0 * p0 + part1 * p1)
            row0, row1 = across_rows(rows, k), across_rows(rows, k + 1)
            if follows:
                next0 = (lower[k] * c - lower[k + 1] * side) * scale
                next1 = (lower[k + 1] * a - lower[k] * side) * scale
                for m in range(k + 2, 8):
                    p0, p1 = picks[m]
                    lower[m] = lower[m] - (next0 * p0 + next1 * p1)
                after = after - (next0 * row0 + next1 * row1)
            rows = rows - (part0 * row0 + part1 * row1)
            first = lax.rsqrt(a)
            ratio = side * (first * first)
            final = jnp.where(sub == k, row0 * first, final)
            final = jnp.where(sub == k + 1, (row1 - row0 * ratio) * (root * (a * first)), final)
            if k == 6:
                if follows: groups[b + 1] = after
            else: yield
        groups[b] = final
        start = b + 2
        if start < count:
            spread = []
            for k in range(0, 8, 2):
                row0, row1 = across_rows(rows, k), across_rows(rows, k + 1)
                lead, side, tail = coefs[k // 2]
                spread += [row0 * tail - row1 * side, row1 * lead - row0 * side]
            far = list(range(b + 2, count))
            whole = [[across_lanes(groups[g], 8 * b + k) for g in far] for k in range(8)]
            for i, g in enumerate(far):
                groups[g] = jnp.where(inside, 0.0, groups[g]) - total_of([whole[k][i] * spread[k] for k in range(8)])
        yield


def split2(x):
    top = x.astype(bf16)
    return top, (x - top.astype(f32)).astype(bf16)


def squares(columns, rows):
    total = None
    for c in range(3):
        offset = columns[:, c : c + 1] - rows[c]
        total = offset * offset if total is None else total + offset * offset
    return total


def outer(left, right):
    return lax.dot_general(
        left, right, (((0,), (0,)), ((), ())), precision=HIGHEST, preferred_element_type=f32
    )


def main_kernel(
    gathered_ref, points_ref, scales_ref, out_ref, matrix, near, tall, signs, solved, stack, ready, lows, done
):
    dims, point_count = points_ref.shape
    rounds = out_ref.shape[0] // 128
    step = 256
    chunks = point_count // step
    weights = [root_factor / jnp.full((1, 128), scales_ref[c], f32) for c in range(dims)]
    flipped = jnp.transpose(gathered_ref[...])
    sub8 = iota((8, 128), 0)
    anchors = []
    for r in range(rounds):
        wide = jnp.zeros((16, 128), f32)
        for s in (2 * r, 2 * r + 1):
            fields = flipped[4 * s : 4 * s + 4, :]
            places = iota((128, fields.shape[1]), 0).astype(f32)
            hot = jnp.where(fields[3:4, :] == places, 1.0, 0.0).astype(bf16)
            parts = split3(fields)
            parts = jnp.concatenate(list(parts) + [parts[0]], 0).astype(bf16)
            wide = wide + lax.dot_general(
                parts, hot, (((1,), (1,)), ((), ())), preferred_element_type=f32
            )
        wide = (wide[0:4, :] + wide[4:8, :]) + wide[8:12, :]
        scaled = [(wide[c : c + 1, :] - 0.5) * weights[c] for c in range(dims)]
        anchors.append(scaled)
        norm = -(scaled[0] * scaled[0] + scaled[1] * scaled[1] + scaled[2] * scaled[2])
        block8 = jnp.where(sub8 == 3, 1.0, jnp.where(sub8 == 4, norm, 0.0))
        for c in range(dims):
            block8 = jnp.where(sub8 == c, scaled[c], block8)
        q1, q2, q3 = split3(block8)
        stood = jnp.transpose(
            jnp.concatenate([q1, q1, q2, q2, q1, q3, q2, q3, block8, jnp.zeros((56, 128), f32)], 0)
        )
        tall[128 * r : 128 * r + 128, :] = stood[:, 64:72]
        signs[128 * r : 128 * r + 128, :] = stood[:, :64].astype(bf16)
    wide8 = (8, point_count)
    here = [(points_ref[c : c + 1, :] - 0.5) * weights[c][:, :1] for c in range(dims)]
    norm = -(here[0] * here[0] + here[1] * here[1] + here[2] * here[2])
    block8 = jnp.where(iota(wide8, 0) == 4, 1.0, jnp.where(iota(wide8, 0) == 3, norm, 0.0))
    for c in range(dims):
        block8 = jnp.where(iota(wide8, 0) == c, here[c] + here[c], block8)
    p1, p2, p3 = split3(block8)
    near[...] = jnp.concatenate([p1, p2, p1, p2, p3, p1, p3, p2], 0).astype(bf16)

    def fill(r, t):
        block = jnp.exp2(-squares(tall[128 * r : 128 * r + 128, :], anchors[t]))
        if t == r:
            diagonal = iota((128, 128), 0) == iota((128, 128), 1)
            block = jnp.where(diagonal, block + nugget_level, block)
        matrix[128 * r : 128 * r + 128, 128 * t : 128 * t + 128] = block

    def block(r, t):
        return matrix[128 * r : 128 * r + 128, 128 * t : 128 * t + 128]

    def columns_task(r, j):
        span = slice(j * step, j * step + step)
        value = jnp.exp2(
            jnp.dot(
                signs[128 * r : 128 * r + 128, :], near[:, span], preferred_element_type=f32
            )
        )
        if r > 0:
            value = value - jnp.dot(
                lows[:, 384 * OFFSET[r] : 384 * (OFFSET[r] + r)],
                stack[: 384 * r, span],
                preferred_element_type=f32,
            )
        top, rest = split2(value)
        ready[:128, span] = top
        ready[128:256, span] = rest
        ready[256:, span] = top

    def solve_task(r, j, inverses):
        span = slice(j * step, j * step + step)
        value = jnp.dot(inverses, ready[:, span], preferred_element_type=f32)
        solved[128 * r : 128 * r + 128, span] = value
        if r < rounds - 1:
            top, rest = split2(value)
            stack[384 * r : 384 * r + 128, span] = top
            stack[384 * r + 128 : 384 * r + 256, span] = rest
            stack[384 * r + 256 : 384 * r + 384, span] = top

    def copy_out(r):
        return pltpu.make_async_copy(
            solved.at[pl.ds(128 * r, 128), :], out_ref.at[pl.ds(128 * r, 128), :], done.at[r]
        )

    def flip_task(s, t):
        top, rest = split2(jnp.transpose(block(s, t)))
        at = 384 * (OFFSET[t] + s)
        lows[:, at : at + 128] = top
        lows[:, at + 128 : at + 256] = top
        lows[:, at + 256 : at + 384] = rest

    def subtract_task(s, t, u):
        matrix[128 * t : 128 * t + 128, 128 * u : 128 * u + 128] = block(t, u) - outer(
            block(s, t), block(s, u)
        )

    keep = iota((128, 128), 0) >= iota((128, 128), 1)
    fill(0, 0)
    inverse = inverses = None
    for r in range(rounds):
        tasks = []
        if r == 0:
            tasks += [functools.partial(fill, t, u) for t in range(rounds) for u in range(t, rounds) if u]
        else:
            s = r - 1
            for u in range(r + 1, rounds):
                tasks.append(functools.partial(widen, s, u, inverse))
            tasks += [functools.partial(flip_task, s, t) for t in range(r, rounds)]
            tasks += [
                functools.partial(subtract_task, s, t, u)
                for t in range(r, rounds)
                for u in range(t, rounds)
                if u > r
            ]
        for j in range(chunks):
            if r > 0:
                tasks.append(functools.partial(solve_task, r - 1, j, inverses))
            tasks.append(functools.partial(columns_task, r, j))
        groups = [matrix[128 * r + 8 * g : 128 * r + 8 * g + 8, 128 * r : 128 * r + 128] for g in range(16)]
        at, slots = 0, 64
        for slot, _ in enumerate(eliminate(groups)):
            until = (slot + 1) * len(tasks) // slots
            while at < until:
                tasks[at]()
                at += 1
        inverse = jnp.where(keep, jnp.concatenate(groups, 0), 0.0)
        top, rest = split2(inverse)
        inverses = jnp.concatenate([top, top, rest], 1)

        def widen(s, u, inverse):
            matrix[128 * s : 128 * s + 128, 128 * u : 128 * u + 128] = jnp.dot(
                inverse, block(s, u), precision=HIGHEST, preferred_element_type=f32
            )

        if r > 0:
            copy_out(r - 1).start()
        if r < rounds - 1:
            widen(r, r + 1, inverse)
            subtract_task(r, r + 1, r + 1)
    for j in range(chunks):
        solve_task(rounds - 1, j, inverses)
    copy_out(rounds - 1).start()
    for r in range(rounds):
        copy_out(r).wait()


OFFSET = [0, 0, 1, 3]


def per_device(points, scales, pivots):
    devices = lax.axis_size(("pts", "rep"))
    dims, point_count = points.shape
    rounds, pivot_count = pivots.shape
    place = lax.axis_index(("pts", "rep")).astype(jnp.int32).reshape(1)
    vmem, smem = pl.BlockSpec(memory_space=pltpu.VMEM), pl.BlockSpec(memory_space=pltpu.SMEM)
    packed = pl.pallas_call(
        pack_kernel,
        out_shape=jax.ShapeDtypeStruct((devices, 128), f32),
        in_specs=[smem, vmem, vmem],
        out_specs=vmem,
    )(place, points, pivots)
    gathered = lax.all_to_all(packed, ("pts", "rep"), 0, 0, tiled=True)
    total = rounds * pivot_count
    return pl.pallas_call(
        main_kernel,
        out_shape=jax.ShapeDtypeStruct((total, point_count), f32),
        in_specs=[vmem, vmem, smem],
        out_specs=pl.BlockSpec(memory_space=pl.ANY),
        scratch_shapes=[
            pltpu.VMEM((total, total), f32),
            pltpu.VMEM((64, point_count), bf16),
            pltpu.VMEM((total, 8), f32),
            pltpu.VMEM((total, 64), bf16),
            pltpu.VMEM((total, point_count), f32),
            pltpu.VMEM((384 * (rounds - 1), point_count), bf16),
            pltpu.VMEM((384, point_count), bf16),
            pltpu.VMEM((128, 384 * 6), bf16),
            pltpu.SemaphoreType.DMA((rounds,)),
        ],
    )(gathered, points, scales)


def solution(mesh):
    placed = (P(None, ("pts", "rep")), P(), P())
    return jax.shard_map(
        per_device, mesh=mesh, in_specs=placed, out_specs=P(None, ("pts", "rep")), check_vma=False
    )
```

```python
import functools
import math

import jax
import jax.numpy as jnp
from jax import lax
from jax.experimental import pallas as pl
from jax.experimental.pallas import tpu as pltpu
from jax.sharding import PartitionSpec as P

nugget_level = 0.1
root_factor = math.sqrt(0.5 * math.log2(math.e))
f32 = jnp.float32
bf16 = jnp.bfloat16
HIGHEST = lax.Precision.HIGHEST


def iota(shape, axis):
    return lax.broadcasted_iota(jnp.int32, shape, axis)


def across_lanes(x, j):
    return jnp.broadcast_to(x[:, j : j + 1], (8, 128))


def across_rows(x, k):
    return jnp.broadcast_to(x[k : k + 1, :], (8, 128))


def pack_kernel(place_ref, points_ref, pivots_ref, out_ref):
    point_count = points_ref.shape[1]
    base = place_ref[0] * point_count
    sub, lane = iota((8, 128), 0), iota((8, 128), 1)
    spread = jnp.zeros((8, 128), jnp.int32)
    for round_index in range(pivots_ref.shape[0]):
        row = jnp.broadcast_to(pivots_ref[round_index : round_index + 1, :], (8, 128))
        spread = jnp.where(sub // 2 == round_index, row, spread)
    local = spread - base
    owned = (local >= 0) & (local < point_count)
    first = jnp.min(jnp.where(owned, lane, 128), axis=1, keepdims=True)
    last = jnp.max(jnp.where(owned, lane, -1), axis=1, keepdims=True)
    second = jnp.where(last > first, last, -1)
    place = jnp.where(sub[:, :1] % 2 == 0, jnp.where(first < 128, first, -1), second)
    here = jnp.sum(jnp.where(lane == place, local, 0), axis=1, keepdims=True)
    columns = iota((8, point_count), 1)
    match = columns == here
    row = jnp.where(lane == 4 * sub + 3, place.astype(f32), 0.0)
    for c in range(points_ref.shape[0]):
        value = jnp.sum(jnp.where(match, points_ref[c : c + 1, :], 0.0), axis=1, keepdims=True)
        row = jnp.where(lane == 4 * sub + c, value, row)
    row = jnp.sum(row, axis=0, keepdims=True)
    out_ref[...] = jnp.broadcast_to(row, out_ref.shape)


def split3(x):
    a = x.astype(bf16).astype(f32)
    rest = x - a
    b = rest.astype(bf16).astype(f32)
    return a, b, rest - b


def total_of(terms):
    while len(terms) > 1:
        terms = [a + b for a, b in zip(terms[::2], terms[1::2])]
    return terms[0]
def total_of(terms):
    while len(terms) > 1:
        terms = [a + b for a, b in zip(terms[::2], terms[1::2])]
    return terms[0]
def eliminate(groups):
    sub, lane = iota((8, 128), 0), iota((8, 128), 1)
    odd = sub % 2 == 1
    pair = sub // 2
    count = len(groups)
    zero = groups[0] * 0.0
    for b in range(count):
        column = [across_lanes(groups[b], 8 * b + k) for k in range(8)]
        column[0], column[1] = column[0] + zero, column[1] + zero
        follows = b < count - 1
        inside = (lane >= 8 * b) & (lane < 8 * b + 8)
        rows = jnp.where(inside, jnp.where(lane - 8 * b == sub, 1.0, 0.0).astype(f32), groups[b])
        if follows:
            lower = [across_lanes(groups[b + 1], 8 * b + k) for k in range(8)]
            after = jnp.where(inside, 0.0, groups[b + 1])
        final = rows
        coefs = []
        for k in range(0, 8, 2):
            mine = pair == k // 2
            a = across_rows(column[k], k)
            side = across_rows(column[k], k + 1)
            c = across_rows(column[k + 1], k + 1)
            root = lax.rsqrt(a * c - side * side)
            scale = root * root
            masked0 = jnp.where(mine, 0.0, column[k])
            masked1 = jnp.where(mine, 0.0, column[k + 1])
            raw0 = masked0 * c - masked1 * side
            raw1 = masked1 * a - masked0 * side
            part0, part1 = raw0 * scale, raw1 * scale
            coefs.append((a * scale, side * scale, c * scale))
            picks = {m: (across_rows(column[k], m), across_rows(column[k + 1], m)) for m in range(k + 2, 8)}
            for m in range(k + 2, 8):
                p0, p1 = picks[m]
                if m < k + 4:
                    column[m] = column[m] - (raw0 * p0 + raw1 * p1) * scale
                else:
                    column[m] = column[m] - (part0 * p0 + part1 * p1)
            row0, row1 = across_rows(rows, k), across_rows(rows, k + 1)
            if follows:
                next0 = (lower[k] * c - lower[k + 1] * side) * scale
                next1 = (lower[k + 1] * a - lower[k] * side) * scale
                for m in range(k + 2, 8):
                    p0, p1 = picks[m]
                    lower[m] = lower[m] - (next0 * p0 + next1 * p1)
                after = after - (next0 * row0 + next1 * row1)
            rows = rows - (part0 * row0 + part1 * row1)
            first = lax.rsqrt(a)
            ratio = side * (first * first)
            final = jnp.where(sub == k, row0 * first, final)
            final = jnp.where(sub == k + 1, (row1 - row0 * ratio) * (root * (a * first)), final)
            if k == 6:
                if follows: groups[b + 1] = after
            else: yield
        groups[b] = final
        start = b + 2
        if start < count:
            spread = []
            for k in range(0, 8, 2):
                row0, row1 = across_rows(rows, k), across_rows(rows, k + 1)
                lead, side, tail = coefs[k // 2]
                spread += [row0 * tail - row1 * side, row1 * lead - row0 * side]
            far = list(range(b + 2, count))
            whole = [[across_lanes(groups[g], 8 * b + k) for g in far] for k in range(8)]
            for i, g in enumerate(far):
                groups[g] = jnp.where(inside, 0.0, groups[g]) - total_of([whole[k][i] * spread[k] for k in range(8)])
        yield


def split2(x):
    top = x.astype(bf16)
    return top, (x - top.astype(f32)).astype(bf16)


def squares(columns, rows):
    total = None
    for c in range(3):
        offset = columns[:, c : c + 1] - rows[c]
        total = offset * offset if total is None else total + offset * offset
    return total


def left_terms(x, axis):
    a, b, c = split3(x)
    return jnp.concatenate([a, a, b, b, a, c], axis).astype(bf16)


def right_terms(y):
    a, b, c = split3(y)
    return jnp.concatenate([a, b, a, b, c, a], 0).astype(bf16)


def outer(left, right):
    return lax.dot_general(
        left_terms(left, 0),
        right_terms(right),
        (((0,), (0,)), ((), ())),
        preferred_element_type=f32,
    )


def main_kernel(
    gathered_ref, points_ref, scales_ref, out_ref, matrix, near, tall, signs, solved, stack, ready, lows,
    inverses, panel, done, last
):
    dims, point_count = points_ref.shape
    rounds = out_ref.shape[0] // 128
    step = 256
    chunks = point_count // step
    weights = [root_factor / jnp.full((1, 128), scales_ref[c], f32) for c in range(dims)]
    flipped = jnp.transpose(gathered_ref[...])
    anchors = {}

    def coordinates(scaled, place, scale):
        wide = (8, scaled[0].shape[1])
        sub = iota(wide, 0)
        norm = -(scaled[0] * scaled[0] + scaled[1] * scaled[1] + scaled[2] * scaled[2])
        block8 = jnp.where(sub == 7 - place, 1.0, jnp.where(sub == place, norm, 0.0))
        for c in range(dims):
            block8 = jnp.where(sub == c, scaled[c] * scale, block8)
        return block8

    def anchor_task(r):
        wide = jnp.zeros((16, 128), f32)
        for s in (2 * r, 2 * r + 1):
            fields = flipped[4 * s : 4 * s + 4, :]
            places = iota((128, fields.shape[1]), 0).astype(f32)
            hot = jnp.where(fields[3:4, :] == places, 1.0, 0.0).astype(bf16)
            parts = split3(fields)
            parts = jnp.concatenate(list(parts) + [parts[0]], 0).astype(bf16)
            wide = wide + lax.dot_general(
                parts, hot, (((1,), (1,)), ((), ())), preferred_element_type=f32
            )
        wide = (wide[0:4, :] + wide[4:8, :]) + wide[8:12, :]
        scaled = [(wide[c : c + 1, :] - 0.5) * weights[c] for c in range(dims)]
        anchors[r] = scaled
        block8 = coordinates(scaled, 4, 1.0)
        q1, q2, q3 = split3(block8)
        stood = jnp.transpose(
            jnp.concatenate([q1, q1, q2, q2, q1, q3, q2, q3, block8, jnp.zeros((56, 128), f32)], 0)
        )
        tall[128 * r : 128 * r + 128, :] = stood[:, 64:72]
        signs[128 * r : 128 * r + 128, :] = stood[:, :64].astype(bf16)

    def near_task(j):
        span = slice(j * 2 * step, (j + 1) * 2 * step)
        here = [(points_ref[c : c + 1, span] - 0.5) * weights[c][:, :1] for c in range(dims)]
        p1, p2, p3 = split3(coordinates(here, 3, 2.0))
        near[:, span] = jnp.concatenate([p1, p2, p1, p2, p3, p1, p3, p2], 0).astype(bf16)

    def fill(r, t):
        block = jnp.exp2(-squares(tall[128 * r : 128 * r + 128, :], anchors[t]))
        if t == r:
            diagonal = iota((128, 128), 0) == iota((128, 128), 1)
            block = jnp.where(diagonal, block + nugget_level, block)
        matrix[128 * r : 128 * r + 128, 128 * t : 128 * t + 128] = block

    def block(r, t):
        return matrix[128 * r : 128 * r + 128, 128 * t : 128 * t + 128]

    def columns_task(r, j):
        span = slice(j * step, j * step + step)
        value = jnp.exp2(
            jnp.dot(
                signs[128 * r : 128 * r + 128, :], near[:, span], preferred_element_type=f32
            )
        )
        if r > 0:
            value = value - jnp.dot(
                lows[:, 384 * OFFSET[r] : 384 * (OFFSET[r] + r)],
                stack[: 384 * r, span],
                preferred_element_type=f32,
            )
        top, rest = split2(value)
        ready[:128, span] = top
        ready[128:256, span] = rest
        ready[256:, span] = top

    def solve_task(r, j):
        span = slice(j * step, j * step + step)
        value = jnp.dot(
            inverses[128 * (r % 2) : 128 * (r % 2) + 128, :],
            ready[:, span],
            preferred_element_type=f32,
        )
        solved[128 * r : 128 * r + 128, span] = value
        if r < rounds - 1:
            top, rest = split2(value)
            stack[384 * r : 384 * r + 128, span] = top
            stack[384 * r + 128 : 384 * r + 256, span] = rest
            stack[384 * r + 256 : 384 * r + 384, span] = top

    def copy_out(r):
        return pltpu.make_async_copy(
            solved.at[pl.ds(128 * r, 128), :], out_ref.at[pl.ds(128 * r, 128), :], done.at[r]
        )

    def copy_last(j):
        rows, columns = pl.ds(128 * (rounds - 1), 128), pl.ds(j * step, step)
        return pltpu.make_async_copy(solved.at[rows, columns], out_ref.at[rows, columns], last.at[j])

    def flip_task(s, t):
        top, rest = split2(jnp.transpose(block(s, t)))
        at = 384 * (OFFSET[t] + s)
        lows[:, at : at + 128] = top
        lows[:, at + 128 : at + 256] = top
        lows[:, at + 256 : at + 384] = rest

    def subtract_task(s, t, u):
        matrix[128 * t : 128 * t + 128, 128 * u : 128 * u + 128] = block(t, u) - outer(
            block(s, t), block(s, u)
        )

    def widen_task(s, u, inverse):
        matrix[128 * s : 128 * s + 128, 128 * u : 128 * u + 128] = jnp.dot(
            left_terms(inverse, 1), right_terms(block(s, u)), preferred_element_type=f32
        )

    def panel_task(r):
        panel[...] = right_terms(block(r, r + 1))

    def quarter_task(r, q, rows):
        lo = 32 * q
        at = 128 * (r % 2) + lo
        top, rest = split2(rows)
        inverses[at : at + 32, :] = jnp.concatenate([top, top, rest], 1)
        if r < rounds - 1:
            wide = jnp.dot(left_terms(rows, 1), panel[...], preferred_element_type=f32)
            matrix[128 * r + lo : 128 * r + lo + 32, 128 * (r + 1) : 128 * (r + 2)] = wide
            after = slice(128 * (r + 1), 128 * (r + 2))
            matrix[after, after] = matrix[after, after] - outer(wide, wide)

    keep = iota((128, 128), 0) >= iota((128, 128), 1)
    anchor_task(0)
    fill(0, 0)
    inverse = None
    task = functools.partial
    for r in range(rounds):
        urgent, tasks = [], []
        if r == 0:
            urgent += [task(anchor_task, 1), task(fill, 0, 1), task(panel_task, 0), task(fill, 1, 1)]
            tasks += [task(near_task, j) for j in range(chunks // 2)]
            tasks += [task(anchor_task, t) for t in range(2, rounds)]
            tasks += [task(fill, t, u) for u in range(2, rounds) for t in range(u + 1)]
        else:
            s = r - 1
            if r < rounds - 1:
                urgent += [task(widen_task, s, r + 1, inverse), task(subtract_task, s, r, r + 1)]
                urgent += [task(panel_task, r), task(subtract_task, s, r + 1, r + 1)]
            urgent.append(task(flip_task, s, r))
            tasks += [task(widen_task, s, u, inverse) for u in range(r + 2, rounds)]
            tasks += [task(flip_task, s, t) for t in range(r + 1, rounds)]
            tasks += [
                task(subtract_task, s, t, u) for t in range(r, rounds) for u in range(max(t, r + 2), rounds)
            ]
        for j in range(chunks):
            if r > 0:
                tasks.append(task(solve_task, r - 1, j))
            tasks.append(task(columns_task, r, j))
        groups = [
            matrix[128 * r + 8 * g : 128 * r + 8 * g + 8, 128 * r : 128 * r + 128] for g in range(16)
        ]
        finished = []
        at = 0
        for slot, _ in enumerate(eliminate(groups)):
            if urgent:
                urgent.pop(0)()
            else:
                share = (slot + 1) / 64
                until = len(tasks) * (SLOPE * share + (1 - SLOPE) * share * share)
                while at < until - 1e-6:
                    tasks[at]()
                    at += 1
            if slot % 16 == 15:
                q = slot // 16
                rows = jnp.where(
                    keep[32 * q : 32 * q + 32, :], jnp.concatenate(groups[4 * q : 4 * q + 4], 0), 0.0
                )
                finished.append(rows)
                quarter_task(r, q, rows)
        inverse = jnp.concatenate(finished, 0)
        if r > 0:
            copy_out(r - 1).start()
    for j in range(chunks):
        solve_task(rounds - 1, j)
        copy_last(j).start()
    for r in range(rounds - 1):
        copy_out(r).wait()
    for j in range(chunks):
        copy_last(j).wait()


SLOPE = 0.5
OFFSET = [0, 0, 1, 3]


def per_device(points, scales, pivots):
    devices = lax.axis_size(("pts", "rep"))
    dims, point_count = points.shape
    rounds, pivot_count = pivots.shape
    place = lax.axis_index(("pts", "rep")).astype(jnp.int32).reshape(1)
    vmem, smem = pl.BlockSpec(memory_space=pltpu.VMEM), pl.BlockSpec(memory_space=pltpu.SMEM)
    packed = pl.pallas_call(
        pack_kernel,
        out_shape=jax.ShapeDtypeStruct((devices, 128), f32),
        in_specs=[smem, vmem, vmem],
        out_specs=vmem,
    )(place, points, pivots)
    gathered = lax.all_to_all(packed, ("pts", "rep"), 0, 0, tiled=True)
    total = rounds * pivot_count
    return pl.pallas_call(
        main_kernel,
        out_shape=jax.ShapeDtypeStruct((total, point_count), f32),
        in_specs=[vmem, vmem, smem],
        out_specs=pl.BlockSpec(memory_space=pl.ANY),
        scratch_shapes=[
            pltpu.VMEM((total, total), f32),
            pltpu.VMEM((64, point_count), bf16),
            pltpu.VMEM((total, 8), f32),
            pltpu.VMEM((total, 64), bf16),
            pltpu.VMEM((total, point_count), f32),
            pltpu.VMEM((384 * (rounds - 1), point_count), bf16),
            pltpu.VMEM((384, point_count), bf16),
            pltpu.VMEM((128, 384 * 6), bf16),
            pltpu.VMEM((256, 384), bf16),
            pltpu.VMEM((768, 128), bf16),
            pltpu.SemaphoreType.DMA((rounds - 1,)),
            pltpu.SemaphoreType.DMA((point_count // 256,)),
        ],
    )(gathered, points, scales)


def solution(mesh):
    placed = (P(None, ("pts", "rep")), P(), P())
    return jax.shard_map(
        per_device, mesh=mesh, in_specs=placed, out_specs=P(None, ("pts", "rep")), check_vma=False
    )
```

```python
import functools
import math

import jax
import jax.numpy as jnp
from jax import lax
from jax.experimental import pallas as pl
from jax.experimental.pallas import tpu as pltpu
from jax.sharding import PartitionSpec as P

nugget_level = 0.1
root_factor = math.sqrt(0.5 * math.log2(math.e))
f32 = jnp.float32
bf16 = jnp.bfloat16
HIGHEST = lax.Precision.HIGHEST


def iota(shape, axis):
    return lax.broadcasted_iota(jnp.int32, shape, axis)


def across_lanes(x, j):
    return jnp.broadcast_to(x[:, j : j + 1], (8, 128))


def across_rows(x, k):
    return jnp.broadcast_to(x[k : k + 1, :], (8, 128))


def pack_kernel(place_ref, points_ref, pivots_ref, out_ref):
    point_count = points_ref.shape[1]
    base = place_ref[0] * point_count
    sub, lane = iota((8, 128), 0), iota((8, 128), 1)
    spread = jnp.zeros((8, 128), jnp.int32)
    for round_index in range(pivots_ref.shape[0]):
        row = jnp.broadcast_to(pivots_ref[round_index : round_index + 1, :], (8, 128))
        spread = jnp.where(sub // 2 == round_index, row, spread)
    local = spread - base
    owned = (local >= 0) & (local < point_count)
    first = jnp.min(jnp.where(owned, lane, 128), axis=1, keepdims=True)
    last = jnp.max(jnp.where(owned, lane, -1), axis=1, keepdims=True)
    second = jnp.where(last > first, last, -1)
    place = jnp.where(sub[:, :1] % 2 == 0, jnp.where(first < 128, first, -1), second)
    here = jnp.sum(jnp.where(lane == place, local, 0), axis=1, keepdims=True)
    columns = iota((8, point_count), 1)
    match = columns == here
    row = jnp.where(lane == 4 * sub + 3, place.astype(f32), 0.0)
    for c in range(points_ref.shape[0]):
        value = jnp.sum(jnp.where(match, points_ref[c : c + 1, :], 0.0), axis=1, keepdims=True)
        row = jnp.where(lane == 4 * sub + c, value, row)
    row = jnp.sum(row, axis=0, keepdims=True)
    out_ref[...] = jnp.broadcast_to(row, out_ref.shape)


def split3(x):
    a = x.astype(bf16).astype(f32)
    rest = x - a
    b = rest.astype(bf16).astype(f32)
    return a, b, rest - b


def total_of(terms):
    while len(terms) > 1:
        terms = [a + b for a, b in zip(terms[::2], terms[1::2])]
    return terms[0]
def total_of(terms):
    while len(terms) > 1:
        terms = [a + b for a, b in zip(terms[::2], terms[1::2])]
    return terms[0]
def eliminate(groups):
    sub, lane = iota((8, 128), 0), iota((8, 128), 1)
    odd = sub % 2 == 1
    pair = sub // 2
    count = len(groups)
    zero = groups[0] * 0.0
    for b in range(count):
        column = [across_lanes(groups[b], 8 * b + k) for k in range(8)]
        column[0], column[1] = column[0] + zero, column[1] + zero
        follows = b < count - 1
        inside = (lane >= 8 * b) & (lane < 8 * b + 8)
        rows = jnp.where(inside, jnp.where(lane - 8 * b == sub, 1.0, 0.0).astype(f32), groups[b])
        if follows:
            lower = [across_lanes(groups[b + 1], 8 * b + k) for k in range(8)]
            after = jnp.where(inside, 0.0, groups[b + 1])
        final = rows
        coefs = []
        for k in range(0, 8, 2):
            mine = pair == k // 2
            a = across_rows(column[k], k)
            side = across_rows(column[k], k + 1)
            c = across_rows(column[k + 1], k + 1)
            root = lax.rsqrt(a * c - side * side)
            scale = root * root
            masked0 = jnp.where(mine, 0.0, column[k])
            masked1 = jnp.where(mine, 0.0, column[k + 1])
            raw0 = masked0 * c - masked1 * side
            raw1 = masked1 * a - masked0 * side
            part0, part1 = raw0 * scale, raw1 * scale
            coefs.append((a * scale, side * scale, c * scale))
            picks = {m: (across_rows(column[k], m), across_rows(column[k + 1], m)) for m in range(k + 2, 8)}
            for m in range(k + 2, 8):
                p0, p1 = picks[m]
                if m < k + 4:
                    column[m] = column[m] - (raw0 * p0 + raw1 * p1) * scale
                else:
                    column[m] = column[m] - (part0 * p0 + part1 * p1)
            row0, row1 = across_rows(rows, k), across_rows(rows, k + 1)
            if follows:
                next0 = (lower[k] * c - lower[k + 1] * side) * scale
                next1 = (lower[k + 1] * a - lower[k] * side) * scale
                for m in range(k + 2, 8):
                    p0, p1 = picks[m]
                    lower[m] = lower[m] - (next0 * p0 + next1 * p1)
                after = after - (next0 * row0 + next1 * row1)
            rows = rows - (part0 * row0 + part1 * row1)
            first = lax.rsqrt(a)
            ratio = side * (first * first)
            final = jnp.where(sub == k, row0 * first, final)
            final = jnp.where(sub == k + 1, (row1 - row0 * ratio) * (root * (a * first)), final)
            if k == 6:
                if follows: groups[b + 1] = after
            else: yield
        groups[b] = final
        start = b + 2
        if start < count:
            spread = []
            for k in range(0, 8, 2):
                row0, row1 = across_rows(rows, k), across_rows(rows, k + 1)
                lead, side, tail = coefs[k // 2]
                spread += [row0 * tail - row1 * side, row1 * lead - row0 * side]
            far = list(range(b + 2, count))
            whole = [[across_lanes(groups[g], 8 * b + k) for g in far] for k in range(8)]
            for i, g in enumerate(far):
                groups[g] = jnp.where(inside, 0.0, groups[g]) - total_of([whole[k][i] * spread[k] for k in range(8)])
        yield


def split2(x):
    top = x.astype(bf16)
    return top, (x - top.astype(f32)).astype(bf16)


def squares(columns, rows):
    total = None
    for c in range(3):
        offset = columns[:, c : c + 1] - rows[c]
        total = offset * offset if total is None else total + offset * offset
    return total


def left_terms(x, axis):
    a, b, c = split3(x)
    return jnp.concatenate([a, a, b, b, a, c], axis).astype(bf16)


def right_terms(y):
    a, b, c = split3(y)
    return jnp.concatenate([a, b, a, b, c, a], 0).astype(bf16)


def outer(left, right):
    return lax.dot_general(
        left_terms(left, 0),
        right_terms(right),
        (((0,), (0,)), ((), ())),
        preferred_element_type=f32,
    )


def main_kernel(
    gathered_ref, points_ref, scales_ref, out_ref, matrix, near, tall, signs, solved, stack, ready, lows,
    inverses, panel, done, last
):
    dims, point_count = points_ref.shape
    rounds = out_ref.shape[0] // 128
    step = 512
    chunks = point_count // step
    weights = [root_factor / jnp.full((1, 128), scales_ref[c], f32) for c in range(dims)]
    flipped = jnp.transpose(gathered_ref[...])
    anchors = {}

    def coordinates(scaled, place, scale):
        wide = (8, scaled[0].shape[1])
        sub = iota(wide, 0)
        norm = -(scaled[0] * scaled[0] + scaled[1] * scaled[1] + scaled[2] * scaled[2])
        block8 = jnp.where(sub == 7 - place, 1.0, jnp.where(sub == place, norm, 0.0))
        for c in range(dims):
            block8 = jnp.where(sub == c, scaled[c] * scale, block8)
        return block8

    def anchor_task(r):
        wide = jnp.zeros((16, 128), f32)
        for s in (2 * r, 2 * r + 1):
            fields = flipped[4 * s : 4 * s + 4, :]
            places = iota((128, fields.shape[1]), 0).astype(f32)
            hot = jnp.where(fields[3:4, :] == places, 1.0, 0.0).astype(bf16)
            parts = split3(fields)
            parts = jnp.concatenate(list(parts) + [parts[0]], 0).astype(bf16)
            wide = wide + lax.dot_general(
                parts, hot, (((1,), (1,)), ((), ())), preferred_element_type=f32
            )
        wide = (wide[0:4, :] + wide[4:8, :]) + wide[8:12, :]
        scaled = [(wide[c : c + 1, :] - 0.5) * weights[c] for c in range(dims)]
        anchors[r] = scaled
        block8 = coordinates(scaled, 4, 1.0)
        q1, q2, q3 = split3(block8)
        stood = jnp.transpose(
            jnp.concatenate([q1, q1, q2, q2, q1, q3, q2, q3, block8, jnp.zeros((56, 128), f32)], 0)
        )
        tall[128 * r : 128 * r + 128, :] = stood[:, 64:72]
        signs[128 * r : 128 * r + 128, :] = stood[:, :64].astype(bf16)

    def near_task(j):
        span = slice(j * step, (j + 1) * step)
        here = [(points_ref[c : c + 1, span] - 0.5) * weights[c][:, :1] for c in range(dims)]
        p1, p2, p3 = split3(coordinates(here, 3, 2.0))
        near[:, span] = jnp.concatenate([p1, p2, p1, p2, p3, p1, p3, p2], 0).astype(bf16)

    def fill(r, t):
        block = jnp.exp2(-squares(tall[128 * r : 128 * r + 128, :], anchors[t]))
        if t == r:
            diagonal = iota((128, 128), 0) == iota((128, 128), 1)
            block = jnp.where(diagonal, block + nugget_level, block)
        matrix[128 * r : 128 * r + 128, 128 * t : 128 * t + 128] = block

    def block(r, t):
        return matrix[128 * r : 128 * r + 128, 128 * t : 128 * t + 128]

    def columns_task(r, j):
        span = slice(j * step, j * step + step)
        value = jnp.exp2(
            jnp.dot(
                signs[128 * r : 128 * r + 128, :], near[:, span], preferred_element_type=f32
            )
        )
        if r > 0:
            value = value - jnp.dot(
                lows[:, 384 * OFFSET[r] : 384 * (OFFSET[r] + r)],
                stack[: 384 * r, span],
                preferred_element_type=f32,
            )
        top, rest = split2(value)
        ready[:128, span] = top
        ready[128:256, span] = rest
        ready[256:, span] = top

    def solve_task(r, j):
        span = slice(j * step, j * step + step)
        value = jnp.dot(
            inverses[128 * (r % 2) : 128 * (r % 2) + 128, :],
            ready[:, span],
            preferred_element_type=f32,
        )
        solved[128 * r : 128 * r + 128, span] = value
        if r < rounds - 1:
            top, rest = split2(value)
            stack[384 * r : 384 * r + 128, span] = top
            stack[384 * r + 128 : 384 * r + 256, span] = rest
            stack[384 * r + 256 : 384 * r + 384, span] = top

    def copy_out(r):
        return pltpu.make_async_copy(
            solved.at[pl.ds(128 * r, 128), :], out_ref.at[pl.ds(128 * r, 128), :], done.at[r]
        )

    def copy_last(j):
        rows, columns = pl.ds(128 * (rounds - 1), 128), pl.ds(j * step, step)
        return pltpu.make_async_copy(solved.at[rows, columns], out_ref.at[rows, columns], last.at[j])

    def flip_task(s, t):
        top, rest = split2(jnp.transpose(block(s, t)))
        at = 384 * (OFFSET[t] + s)
        lows[:, at : at + 128] = top
        lows[:, at + 128 : at + 256] = top
        lows[:, at + 256 : at + 384] = rest

    def subtract_task(s, t, u):
        matrix[128 * t : 128 * t + 128, 128 * u : 128 * u + 128] = block(t, u) - outer(
            block(s, t), block(s, u)
        )

    def widen_task(s, u, inverse):
        matrix[128 * s : 128 * s + 128, 128 * u : 128 * u + 128] = jnp.dot(
            left_terms(inverse, 1), right_terms(block(s, u)), preferred_element_type=f32
        )

    def panel_task(r):
        panel[...] = right_terms(block(r, r + 1))

    def quarter_task(r, q, rows):
        lo = 32 * q
        at = 128 * (r % 2) + lo
        top, rest = split2(rows)
        inverses[at : at + 32, :] = jnp.concatenate([top, top, rest], 1)
        if r < rounds - 1:
            wide = jnp.dot(left_terms(rows, 1), panel[...], preferred_element_type=f32)
            matrix[128 * r + lo : 128 * r + lo + 32, 128 * (r + 1) : 128 * (r + 2)] = wide
            after = slice(128 * (r + 1), 128 * (r + 2))
            matrix[after, after] = matrix[after, after] - outer(wide, wide)

    keep = iota((128, 128), 0) >= iota((128, 128), 1)
    anchor_task(0)
    fill(0, 0)
    inverse = None
    task = functools.partial
    for r in range(rounds):
        urgent, tasks = [], []
        if r == 0:
            urgent += [task(anchor_task, 1), task(fill, 0, 1), task(panel_task, 0), task(fill, 1, 1)]
            tasks += [task(near_task, j) for j in range(chunks)]
            tasks += [task(anchor_task, t) for t in range(2, rounds)]
            tasks += [task(fill, t, u) for u in range(2, rounds) for t in range(u + 1)]
        else:
            s = r - 1
            if r < rounds - 1:
                urgent += [task(widen_task, s, r + 1, inverse), task(subtract_task, s, r, r + 1)]
                urgent += [task(panel_task, r), task(subtract_task, s, r + 1, r + 1)]
            urgent.append(task(flip_task, s, r))
            tasks += [task(widen_task, s, u, inverse) for u in range(r + 2, rounds)]
            tasks += [task(flip_task, s, t) for t in range(r + 1, rounds)]
            tasks += [
                task(subtract_task, s, t, u) for t in range(r, rounds) for u in range(max(t, r + 2), rounds)
            ]
        for j in range(chunks):
            if r > 0:
                tasks.append(task(solve_task, r - 1, j))
            tasks.append(task(columns_task, r, j))
        groups = [
            matrix[128 * r + 8 * g : 128 * r + 8 * g + 8, 128 * r : 128 * r + 128] for g in range(16)
        ]
        finished = []
        at = 0
        for slot, _ in enumerate(eliminate(groups)):
            if urgent:
                urgent.pop(0)()
            else:
                share = (slot + 1) / 64
                until = len(tasks) * (SLOPE * share + (1 - SLOPE) * share * share)
                while at < until - 1e-6:
                    tasks[at]()
                    at += 1
            if slot % 16 == 15:
                q = slot // 16
                rows = jnp.where(
                    keep[32 * q : 32 * q + 32, :], jnp.concatenate(groups[4 * q : 4 * q + 4], 0), 0.0
                )
                finished.append(rows)
                quarter_task(r, q, rows)
        inverse = jnp.concatenate(finished, 0)
        if r > 0:
            copy_out(r - 1).start()
    for j in range(chunks):
        solve_task(rounds - 1, j)
        copy_last(j).start()
    for r in range(rounds - 1):
        copy_out(r).wait()
    for j in range(chunks):
        copy_last(j).wait()


SLOPE = 0.5
OFFSET = [0, 0, 1, 3]


def per_device(points, scales, pivots):
    devices = lax.axis_size(("pts", "rep"))
    dims, point_count = points.shape
    rounds, pivot_count = pivots.shape
    place = lax.axis_index(("pts", "rep")).astype(jnp.int32).reshape(1)
    vmem, smem = pl.BlockSpec(memory_space=pltpu.VMEM), pl.BlockSpec(memory_space=pltpu.SMEM)
    packed = pl.pallas_call(
        pack_kernel,
        out_shape=jax.ShapeDtypeStruct((devices, 128), f32),
        in_specs=[smem, vmem, vmem],
        out_specs=vmem,
    )(place, points, pivots)
    gathered = lax.all_to_all(packed, ("pts", "rep"), 0, 0, tiled=True)
    total = rounds * pivot_count
    return pl.pallas_call(
        main_kernel,
        out_shape=jax.ShapeDtypeStruct((total, point_count), f32),
        in_specs=[vmem, vmem, smem],
        out_specs=pl.BlockSpec(memory_space=pl.ANY),
        scratch_shapes=[
            pltpu.VMEM((total, total), f32),
            pltpu.VMEM((64, point_count), bf16),
            pltpu.VMEM((total, 8), f32),
            pltpu.VMEM((total, 64), bf16),
            pltpu.VMEM((total, point_count), f32),
            pltpu.VMEM((384 * (rounds - 1), point_count), bf16),
            pltpu.VMEM((384, point_count), bf16),
            pltpu.VMEM((128, 384 * 6), bf16),
            pltpu.VMEM((256, 384), bf16),
            pltpu.VMEM((768, 128), bf16),
            pltpu.SemaphoreType.DMA((rounds - 1,)),
            pltpu.SemaphoreType.DMA((point_count // 512,)),
        ],
    )(gathered, points, scales)


def solution(mesh):
    placed = (P(None, ("pts", "rep")), P(), P())
    return jax.shard_map(
        per_device, mesh=mesh, in_specs=placed, out_specs=P(None, ("pts", "rep")), check_vma=False
    )
```
